32 devices in a mesh: row: 4 (over y, x), col: 8 (over z, core).
Axes of the slice: x: 2, y: 2, z: 4, core: 2. Of those that a mesh axis runs over, the one named last changes fastest.
Arguments:
- image: bfloat16 [256, 512, 256], P('row', 'col'), may hold values from -6 to 6
- vert_rate: float32 [8, 256], replicated, may hold values from 0.001171875 to 0.065625
- vert_coef: float32 [8, 256], replicated, may hold values from -28.8 to 28.8
- horiz_rate: float32 [8, 256], replicated, may hold values from 0.0005859375 to 0.065625
- horiz_coef: float32 [8, 256], replicated, may hold values from -28.8 to 28.8
- w_in: bfloat16 [256, 1024], replicated, may hold values from -0.375 to 0.375
- w_out: bfloat16 [1024, 256], replicated, may hold values from -0.1875 to 0.1875
Outputs:
- mixed: bfloat16 [256, 512, 256], P('row', 'col')
The draws below stay inside these ranges and needn't reach their ends.
All inputs are finite; a program needn't handle non-finite values.
Results may differ from the reference program's by a relative error of at most 0.006.
Values sent between devices are 32-bit elements; how exact they have to be, the bound alone decides.
A program may use at most 128 MiB of HBM per device.

```python
import math
import jax
import jax.numpy as jnp
from jax import lax

C = 256
FFN = 1024
MODES = 8
ROWS_DEV = 64
COLS_DEV = 64
NH = 256
NW = 512


def modal_law(key, length, total, salt):
    key = jax.random.fold_in(key, salt)
    keys = jax.random.split(key, 7)
    half = MODES // 2
    slow_lo, slow_hi, base_lo, base_hi, amp_lo, slow_scale = (0.3, 2.0, 0.25, 0.6, 0.3, 0.15)
    slow_rate = jnp.exp(jax.random.uniform(keys[0], (half, C), jnp.float32, math.log(slow_lo), math.log(slow_hi))) / total
    base = jnp.exp(jax.random.uniform(keys[1], (C,), jnp.float32, math.log(base_lo), math.log(base_hi)))
    ratio = jax.random.uniform(keys[2], (half - 1, C), jnp.float32, 1.5, 1.9)
    levels = [base]
    for index in range(half - 1):
        levels.append(levels[-1] * ratio[index])
    mid_rate = jnp.stack(levels, axis=0) / length
    weights = jnp.array([1.0, -3.0, 3.0, -1.0], jnp.float32)
    signs = jnp.where(jax.random.bernoulli(keys[3], 0.5, (C,)), 1.0, -1.0)
    amp = jax.random.uniform(keys[4], (C,), jnp.float32, amp_lo, 0.6) * signs
    mid_gain = jnp.sqrt(1.0 - jnp.exp(-2.0 * mid_rate))
    mid_coef = amp[None, :] * weights[:, None] / mid_gain
    slow_coef = jnp.clip(jax.random.normal(keys[5], (half, C), jnp.float32) * slow_scale, -3.0 * slow_scale, 3.0 * slow_scale)
    rates = jnp.concatenate([slow_rate, mid_rate], axis=0)
    coefs = jnp.concatenate([slow_coef, mid_coef], axis=0)
    order = jax.vmap(lambda single: jax.random.permutation(single, MODES))(jax.random.split(keys[6], C))
    rates = jnp.take_along_axis(rates, order.T, axis=0)
    coefs = jnp.take_along_axis(coefs, order.T, axis=0)
    return (rates.astype(jnp.float32), coefs.astype(jnp.float32))


def draw_vert_rate(key, part):
    return modal_law(key, ROWS_DEV, NH, 11)[0]


def draw_vert_coef(key, part):
    return modal_law(key, ROWS_DEV, NH, 11)[1]


def draw_horiz_rate(key, part):
    return modal_law(key, COLS_DEV, NW, 23)[0]


def draw_horiz_coef(key, part):
    return modal_law(key, COLS_DEV, NW, 23)[1]


def block_scale(rng, extent, cuts, least, largest):
    factor_of = 1.0
    for dim, shards_of in cuts:
        draws = jax.random.uniform(jax.random.fold_in(jax.random.fold_in(rng, 6), dim), (shards_of,), jnp.float32, least / len(cuts), largest / len(cuts))
        factor_of = factor_of * jnp.repeat(jnp.exp(draws), extent[dim] // shards_of).reshape((-1,) + (1,) * (len(extent) - 1 - dim))
    return factor_of


def scatter_about(rng, extent, scale, limit, cuts=(), dtype=jnp.bfloat16):
    drawn = jax.random.normal(rng, extent, jnp.float32) * scale
    if len(cuts) > 0:
        drawn = block_scale(rng, extent, cuts, -0.22, 0.18) * drawn
    return jnp.clip(drawn, min=-limit, max=limit).astype(dtype)


def setup_inputs(seed: int = 0) -> dict:
    splits = jax.random.split(jax.random.key(seed), 8)
    image = scatter_about(splits[0], (NH, NW, C), 1.0, 6.0, ((0, 4), (1, 8)))
    vert_rate = draw_vert_rate(jax.random.fold_in(splits[7], 71), 0)
    vert_coef = draw_vert_coef(jax.random.fold_in(splits[7], 71), 0)
    horiz_rate = draw_horiz_rate(jax.random.fold_in(splits[7], 71), 0)
    horiz_coef = draw_horiz_coef(jax.random.fold_in(splits[7], 71), 0)
    w_in = scatter_about(splits[5], (C, FFN), C ** -0.5, 0.375)
    w_out = scatter_about(splits[6], (FFN, C), FFN ** -0.5, 0.1875)
    return {"image": image, "vert_rate": vert_rate, "vert_coef": vert_coef, "horiz_rate": horiz_rate, "horiz_coef": horiz_coef, "w_in": w_in, "w_out": w_out}


def modal_scan(field, rate, coef):
    pole = jnp.exp(-rate)
    gain = jnp.sqrt(1.0 - pole * pole)
    state0 = jnp.zeros((rate.shape[0], field.shape[1], field.shape[2]), jnp.float32)

    def advance(state, line):
        state = pole[:, None, :] * state + gain[:, None, :] * line[None, :, :]
        return (state, lax.optimization_barrier(jnp.sum(coef[:, None, :] * state, axis=0)))
    _, result = lax.scan(advance, state0, field)
    return result

def reference(image, vert_rate, vert_coef, horiz_rate, horiz_coef, w_in, w_out):
    vert = modal_scan(image.astype(jnp.float32), vert_rate, vert_coef)
    act = jax.nn.gelu(vert).astype(jnp.bfloat16)
    horiz = jnp.transpose(modal_scan(jnp.transpose(act.astype(jnp.float32), (1, 0, 2)), horiz_rate, horiz_coef), (1, 0, 2))

    def one_row(line):
        normed = (line * lax.rsqrt(lax.optimization_barrier(jnp.mean(line * line, axis=-1, keepdims=True)) + 1e-06)).astype(jnp.bfloat16)
        hidden = jax.nn.gelu(jnp.dot(normed, w_in, preferred_element_type=jnp.float32)).astype(jnp.bfloat16)
        return (line + jnp.dot(hidden, w_out, preferred_element_type=jnp.float32)).astype(jnp.bfloat16)
    return lax.map(one_row, horiz)
```

```python
import functools

import jax
import jax.numpy as jnp
from jax import lax
from jax.experimental import pallas as pl
from jax.experimental.pallas import tpu as pltpu
from jax.sharding import PartitionSpec as P

LANES = 128
GROUP = 16
BLOCK = 16
AHEAD = 3
PIECES = 2
MESH = pl.DeviceIdType.MESH
C0 = 0.7978845608028654
C1 = 0.7978845608028654 * 0.044715


def twice_gelu(x):
    return x + x * jnp.tanh(x * (C0 + C1 * (x * x)))


def layer_kernel(
    nrow, ncol, rows, cols, modes, halves,
    image_hbm, vrate_hbm, vcoef_hbm, hrate_hbm, hcoef_hbm, w_in_hbm, w_out_hbm, half,
    img, vrate, vcoef, hrate, hcoef, w_in, w_out, out,
    ptab, qtab, dtab, lead, vedge, vin, hedge, hin,
    vsend, vrecv, hsend, hrecv, img_sem, arg_sem, out_sem,
):
    row = lax.axis_index("row")
    col = lax.axis_index("col")
    nk = cols // GROUP
    nr = rows // GROUP
    pitch = cols + 1
    size = rows * pitch

    def fetch_image(k):
        part = pl.ds(pl.multiple_of(k * GROUP, GROUP), GROUP)
        return pltpu.make_async_copy(image_hbm.at[:, part, :], img.at[:, part, :], img_sem.at[k])

    fetches = [
        pltpu.make_async_copy(src, dst, arg_sem.at[i])
        for i, (src, dst) in enumerate((
            (vrate_hbm, vrate), (vcoef_hbm, vcoef), (hrate_hbm, hrate), (hcoef_hbm, hcoef),
            (w_in_hbm, w_in), (w_out_hbm, w_out),
        ))
    ]
    for copy in fetches[:4]:
        copy.start()
    for k in range(nk):
        fetch_image(k).start()
    for copy in fetches[4:]:
        copy.start()

    barrier = pltpu.get_barrier_semaphore()
    neighbours = (
        (row > 0, {"row": row - 1}),
        (row < nrow - 1, {"row": row + 1}),
        (col > 0, {"col": col - 1}),
        (col < ncol - 1, {"col": col + 1}),
    )
    for there, device in neighbours:
        @pl.when(there)
        def _():
            pl.semaphore_signal(barrier, inc=1, device_id=device, device_id_type=MESH)

    for copy in fetches[:4]:
        copy.wait()

    for axis, (rate, coef, length) in enumerate(((vrate, vcoef, rows), (hrate, hcoef, cols))):
        for h in range(halves):
            r = rate[:, h * LANES:(h + 1) * LANES]
            gain = jnp.sqrt(1.0 - jnp.exp(-2.0 * r))
            q = coef[:, h * LANES:(h + 1) * LANES] * gain
            ptab[axis, h] = jnp.exp(-r)
            qtab[axis, h] = q
            dtab[axis, h] = jnp.exp(-r * length)

    def fill_lead():
        for axis, (rate, length) in enumerate(((vrate, rows), (hrate, cols))):

            def fill(i, carry):
                for h in range(halves):
                    r = rate[:, h * LANES:(h + 1) * LANES]
                    q = qtab[axis, h]
                    for j in range(modes):
                        t = i * modes + j
                        power = jnp.exp(-r * (t + 1).astype(jnp.float32))
                        lead[axis, h, pl.ds(pl.multiple_of(t * modes, modes), modes), :] = q * power
                return carry

            lax.fori_loop(0, length // modes, fill, 0)

    def spread(tab, axis, h):
        block = tab[axis, h]
        return [jnp.broadcast_to(block[m:m + 1, :], (GROUP, LANES)) for m in range(modes)]

    def total(terms):
        while len(terms) > 1:
            terms = [a + b for a, b in zip(terms[::2], terms[1::2])] + terms[len(terms) & ~1:]
        return terms[0]

    def vcopy(g, i):
        part = pl.ds(i * (modes // PIECES), modes // PIECES)
        return pltpu.make_async_remote_copy(
            src_ref=vedge.at[g, part], dst_ref=vin.at[g, part],
            send_sem=vsend.at[g * PIECES + i], recv_sem=vrecv.at[g * PIECES + i],
            device_id={"row": row + 1}, device_id_type=MESH,
        )

    def hcopy(g, i):
        part = pl.ds(i * (modes // PIECES), modes // PIECES)
        return pltpu.make_async_remote_copy(
            src_ref=hedge.at[g, part], dst_ref=hin.at[g, part],
            send_sem=hsend.at[g * PIECES + i], recv_sem=hrecv.at[g * PIECES + i],
            device_id={"col": col + 1}, device_id_type=MESH,
        )

    def local(g):
        h, k = g // nk, g % nk

        @pl.when(h == 0)
        def _():
            fetch_image(k).wait()

        p, q = spread(ptab, 0, h), spread(qtab, 0, h)
        lane = pl.multiple_of(h * LANES, LANES)
        first = pl.multiple_of(k * GROUP, GROUP)

        def step(t, state):
            u = img[t, pl.ds(first, GROUP), pl.ds(lane, LANES)].astype(jnp.float32)
            state = tuple(p[m] * state[m] + u for m in range(modes))
            y = total([q[m] * state[m] for m in range(modes)])
            out[pl.ds(h * size + t * pitch + first, GROUP), :] = y
            return state

        zero = jnp.zeros((GROUP, LANES), jnp.float32)
        state = lax.fori_loop(0, rows, step, (zero,) * modes, unroll=4)
        for m in range(modes):
            vedge[g, m] = state[m]

    def enter(axis, g, h, place, count, edge, incoming, copy):
        for i in range(PIECES):
            @pl.when(place > 0)
            def _():
                copy(g, i).wait_recv()

            @pl.when(jnp.logical_and(place > 0, place < count - 1))
            def _():
                d = dtab[axis, h]
                for m in range(i * (modes // PIECES), (i + 1) * (modes // PIECES)):
                    edge[g, m] = jnp.broadcast_to(d[m:m + 1, :], (GROUP, LANES)) * incoming[g, m] + edge[g, m]
                copy(g, i).start()

    def enter_rows(g):
        enter(0, g, g // nk, row, nrow, vedge, vin, vcopy)

    def finish_rows(g):
        h, k = g // nk, g % nk
        first = pl.multiple_of(k * GROUP, GROUP)
        carried = [vin[g, m] for m in range(modes)]

        def correct(t, carry):
            at = pl.ds(h * size + t * pitch + first, GROUP)
            here = lead[0, h, pl.ds(pl.multiple_of(t * modes, modes), modes), :]
            y = out[at, :] + total([here[m:m + 1, :] * carried[m] for m in range(modes)])
            act = (0.5 * twice_gelu(y)).astype(jnp.bfloat16)
            out[at, :] = act.astype(jnp.float32)
            return carry

        lax.fori_loop(0, rows, correct, 0, unroll=8)
        p, q = spread(ptab, 1, h), spread(qtab, 1, h)

        def group(j, carry):
            c = h * nr + j
            base = h * size + j * (GROUP * pitch) + first

            def step(t, state):
                at = pl.ds(base + t, GROUP, stride=pitch)
                u = out[at, :]
                state = tuple(p[m] * state[m] + u for m in range(modes))
                out[at, :] = total([q[m] * state[m] for m in range(modes)])
                return state

            state = lax.fori_loop(0, GROUP, step, tuple(hedge[c, m] for m in range(modes)), unroll=4)
            for m in range(modes):
                hedge[c, m] = state[m]

            @pl.when(jnp.logical_and(k == nk - 1, jnp.logical_and(col == 0, ncol > 1)))
            def _():
                for i in range(PIECES):
                    hcopy(c, i).start()

            return carry

        lax.fori_loop(0, nr, group, 0)

    def enter_cols(c):
        enter(1, c, c // nr, col, ncol, hedge, hin, hcopy)

    def finish_cols(c):
        h, j = c // nr, c % nr

        @pl.when(col > 0)
        def _():
            carried = [hin[c, m] for m in range(modes)]
            base = h * size + j * (GROUP * pitch)

            def correct(t, carry):
                at = pl.ds(base + t, GROUP, stride=pitch)
                here = lead[1, h, pl.ds(pl.multiple_of(t * modes, modes), modes), :]
                out[at, :] = out[at, :] + total([here[m:m + 1, :] * carried[m] for m in range(modes)])
                return carry

            lax.fori_loop(0, cols, correct, 0, unroll=8)

    def mlp(i):
        line = jnp.concatenate(
            [
                jnp.concatenate([out[pl.ds(h * size + (i * BLOCK + r) * pitch, cols), :] for h in range(halves)], axis=1)
                for r in range(BLOCK)
            ],
            axis=0,
        )
        scale = lax.rsqrt(jnp.mean(line * line, axis=-1, keepdims=True) + 1e-06)
        normed = (line * scale).astype(jnp.bfloat16)
        pre = jnp.dot(normed, w_in[...], preferred_element_type=jnp.float32).astype(jnp.bfloat16)
        hidden = twice_gelu(pre)
        result = line + 0.5 * jnp.dot(hidden, w_out[...], preferred_element_type=jnp.float32)
        half[pl.ds(pl.multiple_of(i * (BLOCK * cols), BLOCK * cols), BLOCK * cols), :] = result.astype(half.dtype)

    def store(i):
        part = pl.ds(pl.multiple_of(i * (BLOCK * cols), BLOCK * cols), BLOCK * cols)
        return pltpu.make_async_copy(half.at[part], half_hbm.at[part], out_sem.at[i])

    hedge[...] = jnp.zeros_like(hedge)

    @pl.when(row == 0)
    def _():
        vin[...] = jnp.zeros_like(vin)

    pl.semaphore_wait(barrier, sum(jnp.where(there, 1, 0) for there, _ in neighbours))

    chunks = halves * nk
    strips = halves * nr

    def scan(s, carry):
        local(s)

        @pl.when(jnp.logical_and(row == 0, nrow > 1))
        def _():
            for i in range(PIECES):
                vcopy(s, i).start()

        @pl.when(jnp.logical_and(row == 1, s >= chunks - AHEAD))
        def _():
            enter_rows(s - (chunks - AHEAD))

        return carry

    lax.fori_loop(0, chunks, scan, 0)
    fill_lead()

    def main(g, carry):
        @pl.when(row != 1)
        def _():
            enter_rows(g)

        finish_rows(g)

        @pl.when(jnp.logical_and(row == 1, g + AHEAD < chunks))
        def _():
            enter_rows(g + AHEAD)

        @pl.when(g >= nk + col)
        def _():
            enter_cols(g - nk - col)
            finish_cols(g - nk - col)

        return carry

    lax.fori_loop(0, chunks, main, 0)
    early = (halves - 1) * nr

    def middle(c, carry):
        enter_cols(c)
        finish_cols(c)
        return carry

    lax.fori_loop(jnp.maximum(chunks - nk - col, 0), early, middle, 0)
    for copy in fetches[4:]:
        copy.wait()

    @pl.when(col < ncol - 1)
    def _():
        def relay(c, carry):
            enter_cols(c)
            return carry

        lax.fori_loop(early, strips, relay, 0)

    def last(c, carry):
        @pl.when(col == ncol - 1)
        def _():
            enter_cols(c)

        finish_cols(c)

        def block(i, carry):
            mlp(i)
            return carry

        per = GROUP // BLOCK
        lax.fori_loop((c - early) * per, (c - early + 1) * per, block, 0)
        return carry

    lax.fori_loop(early, strips, last, 0)

    def drain(g, carry):
        @pl.when(row < nrow - 1)
        def _():
            for i in range(PIECES):
                vcopy(g, i).wait_send()

        return carry

    lax.fori_loop(0, chunks, drain, 0)

    def drain_cols(g, carry):
        @pl.when(col < ncol - 1)
        def _():
            for i in range(PIECES):
                hcopy(g, i).wait_send()

        return carry

    lax.fori_loop(0, strips, drain_cols, 0)


def emit(src, dst, sem):
    copy = pltpu.make_async_copy(src, dst, sem.at[0])
    copy.start()
    copy.wait()


def on_device(nrow, ncol, image, vert_rate, vert_coef, horiz_rate, horiz_coef, w_in, w_out):
    rows, cols, channels = image.shape
    modes = vert_rate.shape[0]
    halves = channels // LANES
    chunks, strips = halves * (cols // GROUP), halves * (rows // GROUP)
    f32 = jnp.float32
    args = (image, vert_rate, vert_coef, horiz_rate, horiz_coef, w_in, w_out)
    half = pl.pallas_call(
        functools.partial(layer_kernel, nrow, ncol, rows, cols, modes, halves),
        out_shape=pltpu.VMEM((rows * cols, channels), jnp.bfloat16),
        in_specs=[pl.BlockSpec(memory_space=pltpu.MemorySpace.HBM)] * len(args),
        out_specs=pl.BlockSpec(memory_space=pltpu.MemorySpace.VMEM),
        scratch_shapes=[pltpu.VMEM(a.shape, a.dtype) for a in args] + [
            pltpu.VMEM((halves * rows * (cols + 1), LANES), f32),
            pltpu.VMEM((2, halves, modes, LANES), f32),
            pltpu.VMEM((2, halves, modes, LANES), f32),
            pltpu.VMEM((2, halves, modes, LANES), f32),
            pltpu.VMEM((2, halves, max(rows, cols) * modes, LANES), f32),
            pltpu.VMEM((chunks, modes, GROUP, LANES), f32),
            pltpu.VMEM((chunks, modes, GROUP, LANES), f32),
            pltpu.VMEM((strips, modes, GROUP, LANES), f32),
            pltpu.VMEM((strips, modes, GROUP, LANES), f32),
            pltpu.SemaphoreType.DMA((chunks * PIECES,)),
            pltpu.SemaphoreType.DMA((chunks * PIECES,)),
            pltpu.SemaphoreType.DMA((strips * PIECES,)),
            pltpu.SemaphoreType.DMA((strips * PIECES,)),
            pltpu.SemaphoreType.DMA((cols // GROUP,)),
            pltpu.SemaphoreType.DMA((6,)),
            pltpu.SemaphoreType.DMA((rows // BLOCK,)),
        ],
        compiler_params=pltpu.CompilerParams(collective_id=0, has_side_effects=True, vmem_limit_bytes=67043328 - rows * cols * channels * 2 - 4096),
    )(*args)
    full = pl.pallas_call(
        emit, out_shape=jax.ShapeDtypeStruct((rows * cols, channels), jnp.bfloat16),
        in_specs=[pl.BlockSpec(memory_space=pltpu.MemorySpace.VMEM)],
        out_specs=pl.BlockSpec(memory_space=pltpu.MemorySpace.HBM),
        scratch_shapes=[pltpu.SemaphoreType.DMA((1,))],
        compiler_params=pltpu.CompilerParams(vmem_limit_bytes=1000000),
    )(half)
    return full.reshape(rows, cols, channels)


def solution(mesh):
    placed = (P("row", "col", None), P(), P(), P(), P(), P(), P())
    return jax.shard_map(
        functools.partial(on_device, mesh.shape["row"], mesh.shape["col"]),
        mesh=mesh, in_specs=placed, out_specs=P("row", "col", None), check_vma=False,
    )
```

```python
import functools

import jax
import jax.numpy as jnp
from jax import lax
from jax.experimental import pallas as pl
from jax.experimental.pallas import tpu as pltpu
from jax.sharding import PartitionSpec as P

LANES = 128
GROUP = 16
BLOCK = 16
AHEAD = 2
PIECES = 2
MESH = pl.DeviceIdType.MESH
C0 = 0.7978845608028654
C1 = 0.7978845608028654 * 0.044715


def twice_gelu(x):
    return x + x * jnp.tanh(x * (C0 + C1 * (x * x)))


def layer_kernel(
    nrow, ncol, rows, cols, modes, halves,
    image_hbm, vrate_hbm, vcoef_hbm, hrate_hbm, hcoef_hbm, w_in_hbm, w_out_hbm, half,
    img, vrate, vcoef, hrate, hcoef, w_in, w_out, out,
    ptab, qtab, vdt, vdp, hdt, lead, vtot, vin, vpre, hedge, hpart, hsum, hin, hcar,
    vsend, vrecv, asend, arecv, csend, crecv, fsend, frecv, img_sem, arg_sem,
):
    row = lax.axis_index("row")
    col = lax.axis_index("col")
    nk = cols // GROUP
    nr = rows // GROUP
    pitch = cols + 1
    size = rows * pitch
    steps = row_steps(nrow)
    pair = pair_of(ncol)
    core, z, nz = col % pair, col // pair, ncol // pair
    chunks = halves * nk
    strips = halves * nr
    early = (halves - 1) * nr
    both = jnp.logical_and

    def fetch_image(k):
        part = pl.ds(pl.multiple_of(k * GROUP, GROUP), GROUP)
        return pltpu.make_async_copy(image_hbm.at[:, part, :], img.at[:, part, :], img_sem.at[k])

    fetches = [
        pltpu.make_async_copy(src, dst, arg_sem.at[i])
        for i, (src, dst) in enumerate((
            (vrate_hbm, vrate), (vcoef_hbm, vcoef), (hrate_hbm, hrate), (hcoef_hbm, hcoef),
            (w_in_hbm, w_in), (w_out_hbm, w_out),
        ))
    ]
    for copy in fetches[:4]:
        copy.start()
    for k in range(nk):
        fetch_image(k).start()
    for copy in fetches[4:]:
        copy.start()

    def bit_of(s):
        return (row // (1 << s)) % 2

    def row_partner(s):
        return row + (1 << s) * (1 - 2 * bit_of(s))

    def later(s):
        return row // (1 << s) != (nrow >> s) - 1

    barrier = pltpu.get_barrier_semaphore()
    always = row >= 0
    neighbours = [(always, {"row": row_partner(s)}) for s in range(steps)]
    if pair == 2:
        neighbours.append((always, {"col": col + 1 - 2 * core}))
    if nz > 1:
        neighbours.append((z > 0, {"col": col - pair}))
        neighbours.append((z < nz - 1, {"col": col + pair}))
    for there, device in neighbours:
        @pl.when(there)
        def _():
            pl.semaphore_signal(barrier, inc=1, device_id=device, device_id_type=MESH)

    for copy in fetches[:4]:
        copy.wait()

    for axis, (rate, coef) in enumerate(((vrate, vcoef), (hrate, hcoef))):
        for h in range(halves):
            r = rate[:, h * LANES:(h + 1) * LANES]
            gain = jnp.sqrt(1.0 - jnp.exp(-2.0 * r))
            ptab[axis, h] = jnp.exp(-r)
            qtab[axis, h] = coef[:, h * LANES:(h + 1) * LANES] * gain

    for h in range(halves):
        r = vrate[:, h * LANES:(h + 1) * LANES]
        for s in range(steps):
            vdt[s, h] = jnp.exp(-r * (rows << s))
            vdp[s, h] = jnp.exp(-r * (rows * (row % (1 << s))).astype(jnp.float32))
        r = hrate[:, h * LANES:(h + 1) * LANES]
        hdt[0, h] = jnp.exp(-r * cols)
        hdt[1, h] = jnp.exp(-r * (cols * pair))

    def fill_lead():
        for axis, (rate, length) in enumerate(((vrate, rows), (hrate, cols))):

            def fill(i, carry):
                for h in range(halves):
                    r = rate[:, h * LANES:(h + 1) * LANES]
                    q = qtab[axis, h]
                    for j in range(modes):
                        t = i * modes + j
                        power = jnp.exp(-r * (t + 1).astype(jnp.float32))
                        lead[axis, h, pl.ds(pl.multiple_of(t * modes, modes), modes), :] = q * power
                return carry

            lax.fori_loop(0, length // modes, fill, 0)

    def spread(tab, axis, h):
        block = tab[axis, h]
        return [jnp.broadcast_to(block[m:m + 1, :], (GROUP, LANES)) for m in range(modes)]

    def total(terms):
        while len(terms) > 1:
            terms = [a + b for a, b in zip(terms[::2], terms[1::2])] + terms[len(terms) & ~1:]
        return terms[0]

    def span(i):
        return range(i * (modes // PIECES), (i + 1) * (modes // PIECES))

    def vcopy(s, g, i):
        part = pl.ds(i * (modes // PIECES), modes // PIECES)
        return pltpu.make_async_remote_copy(
            src_ref=vtot.at[s, g, part], dst_ref=vin.at[s, g, part],
            send_sem=vsend.at[s, g * PIECES + i], recv_sem=vrecv.at[s, g * PIECES + i],
            device_id={"row": row_partner(s)}, device_id_type=MESH,
        )

    def join_copy(c):
        return pltpu.make_async_remote_copy(
            src_ref=hedge.at[c], dst_ref=hpart.at[c], send_sem=asend.at[c], recv_sem=arecv.at[c],
            device_id={"col": col + 1 - 2 * core}, device_id_type=MESH,
        )

    def chain_copy(c, i):
        part = pl.ds(i * (modes // PIECES), modes // PIECES)
        return pltpu.make_async_remote_copy(
            src_ref=hsum.at[c, part], dst_ref=hin.at[c, part],
            send_sem=csend.at[c * PIECES + i], recv_sem=crecv.at[c * PIECES + i],
            device_id={"col": col + pair}, device_id_type=MESH,
        )

    def forward_copy(src, c):
        return pltpu.make_async_remote_copy(
            src_ref=src.at[c], dst_ref=hin.at[c], send_sem=fsend.at[c], recv_sem=frecv.at[c],
            device_id={"col": col + 1 - 2 * core}, device_id_type=MESH,
        )

    def owner(c):
        return c % pair == core

    def local(g):
        h, k = g // nk, g % nk

        @pl.when(h == 0)
        def _():
            fetch_image(k).wait()

        p, q = spread(ptab, 0, h), spread(qtab, 0, h)
        lane = pl.multiple_of(h * LANES, LANES)
        first = pl.multiple_of(k * GROUP, GROUP)

        def step(t, state):
            u = img[t, pl.ds(first, GROUP), pl.ds(lane, LANES)].astype(jnp.float32)
            state = tuple(p[m] * state[m] + u for m in range(modes))
            y = total([q[m] * state[m] for m in range(modes)])
            out[pl.ds(h * size + t * pitch + first, GROUP), :] = y
            return state

        zero = jnp.zeros((GROUP, LANES), jnp.float32)
        state = lax.fori_loop(0, rows, step, (zero,) * modes, unroll=4)
        for m in range(modes):
            vtot[0, g, m] = state[m]

    def decay(tab, s, h, m):
        return jnp.broadcast_to(tab[s, h][m:m + 1, :], (GROUP, LANES))

    def exchange(s, g):
        h = g // nk
        bit = bit_of(s)
        onward = later(s + 1)
        for i in range(PIECES):
            @pl.when(jnp.logical_or(bit == 1, onward))
            def _():
                vcopy(s, g, i).wait_recv()

            if s + 1 < steps:
                @pl.when(onward)
                def _():
                    for m in span(i):
                        mine, theirs = vtot[s, g, m], vin[s, g, m]
                        older = jnp.where(bit == 0, mine, theirs)
                        newer = jnp.where(bit == 0, theirs, mine)
                        vtot[s + 1, g, m] = decay(vdt, s, h, m) * older + newer
                    vcopy(s + 1, g, i).start()

            @pl.when(bit == 1)
            def _():
                for m in span(i):
                    vpre[g, m] = decay(vdp, s, h, m) * vin[s, g, m] + vpre[g, m]

    def finish_rows(g):
        h, k = g // nk, g % nk
        first = pl.multiple_of(k * GROUP, GROUP)
        carried = [vpre[g, m] for m in range(modes)]

        def correct(t, carry):
            at = pl.ds(h * size + t * pitch + first, GROUP)
            here = lead[0, h, pl.ds(pl.multiple_of(t * modes, modes), modes), :]
            y = out[at, :] + total([here[m:m + 1, :] * carried[m] for m in range(modes)])
            act = (0.5 * twice_gelu(y)).astype(jnp.bfloat16)
            out[at, :] = act.astype(jnp.float32)
            return carry

        lax.fori_loop(0, rows, correct, 0, unroll=8)
        p, q = spread(ptab, 1, h), spread(qtab, 1, h)

        def group(j, carry):
            c = h * nr + j
            base = h * size + j * (GROUP * pitch) + first

            def step(t, state):
                at = pl.ds(base + t, GROUP, stride=pitch)
                u = out[at, :]
                state = tuple(p[m] * state[m] + u for m in range(modes))
                out[at, :] = total([q[m] * state[m] for m in range(modes)])
                return state

            state = lax.fori_loop(0, GROUP, step, tuple(hedge[c, m] for m in range(modes)), unroll=4)
            for m in range(modes):
                hedge[c, m] = state[m]

            if pair == 2:
                @pl.when(both(k == nk - 1, jnp.logical_not(owner(c))))
                def _():
                    join_copy(c).start()

            return carry

        lax.fori_loop(0, nr, group, 0)

    def join(c):
        h = c // nr

        @pl.when(owner(c))
        def _():
            if pair == 2:
                join_copy(c).wait_recv()
            for m in range(modes):
                mine = hedge[c, m]
                if pair == 2:
                    theirs = hpart[c, m]
                    older = jnp.where(core == 0, mine, theirs)
                    newer = jnp.where(core == 0, theirs, mine)
                    mine = decay(hdt, 0, h, m) * older + newer
                hsum[c, m] = mine
            if nz > 1:
                @pl.when(z == 0)
                def _():
                    for i in range(PIECES):
                        chain_copy(c, i).start()
            if pair == 2:
                @pl.when(col == 0)
                def _():
                    forward_copy(hedge, c).start()

    def enter(c):
        h = c // nr

        @pl.when(both(owner(c), z > 0))
        def _():
            for i in range(PIECES):
                chain_copy(c, i).wait_recv()

                @pl.when(z < nz - 1)
                def _():
                    for m in span(i):
                        hsum[c, m] = decay(hdt, 1, h, m) * hin[c, m] + hsum[c, m]
                    chain_copy(c, i).start()

            if pair == 2:
                @pl.when(core == 0)
                def _():
                    for m in range(modes):
                        hpart[c, m] = decay(hdt, 0, h, m) * hin[c, m] + hedge[c, m]
                    forward_copy(hpart, c).start()
                    for m in range(modes):
                        hcar[c, m] = hin[c, m]

                @pl.when(core == 1)
                def _():
                    forward_copy(hin, c).start()
                    for m in range(modes):
                        hcar[c, m] = decay(hdt, 0, h, m) * hin[c, m] + hpart[c, m]
            else:
                for m in range(modes):
                    hcar[c, m] = hin[c, m]

        if pair == 2:
            @pl.when(both(owner(c), col == 1))
            def _():
                for m in range(modes):
                    hcar[c, m] = hpart[c, m]

            @pl.when(both(jnp.logical_not(owner(c)), col > 0))
            def _():
                forward_copy(hin, c).wait_recv()
                for m in range(modes):
                    hcar[c, m] = hin[c, m]

    def finish_cols(c):
        h, j = c // nr, c % nr

        @pl.when(col > 0)
        def _():
            carried = [hcar[c, m] for m in range(modes)]
            base = h * size + j * (GROUP * pitch)

            def correct(t, carry):
                at = pl.ds(base + t, GROUP, stride=pitch)
                here = lead[1, h, pl.ds(pl.multiple_of(t * modes, modes), modes), :]
                out[at, :] = out[at, :] + total([here[m:m + 1, :] * carried[m] for m in range(modes)])
                return carry

            lax.fori_loop(0, cols, correct, 0, unroll=8)

    def mlp(i):
        line = jnp.concatenate(
            [
                jnp.concatenate([out[pl.ds(h * size + (i * BLOCK + r) * pitch, cols), :] for h in range(halves)], axis=1)
                for r in range(BLOCK)
            ],
            axis=0,
        )
        scale = lax.rsqrt(jnp.mean(line * line, axis=-1, keepdims=True) + 1e-06)
        normed = (line * scale).astype(jnp.bfloat16)
        pre = jnp.dot(normed, w_in[...], preferred_element_type=jnp.float32).astype(jnp.bfloat16)
        hidden = twice_gelu(pre)
        result = line + 0.5 * jnp.dot(hidden, w_out[...], preferred_element_type=jnp.float32)
        half[pl.ds(pl.multiple_of(i * (BLOCK * cols), BLOCK * cols), BLOCK * cols), :] = result.astype(half.dtype)

    hedge[...] = jnp.zeros_like(hedge)
    vpre[...] = jnp.zeros_like(vpre)

    pl.semaphore_wait(barrier, sum(jnp.where(there, 1, 0) for there, _ in neighbours))

    def scan(s, carry):
        local(s)
        if steps:
            @pl.when(later(0))
            def _():
                for i in range(PIECES):
                    vcopy(0, s, i).start()

            @pl.when(s >= chunks - AHEAD)
            def _():
                exchange(0, s - (chunks - AHEAD))

        return carry

    lax.fori_loop(0, chunks, scan, 0)
    fill_lead()

    def main(g, carry):
        for s in range(1, steps):
            exchange(s, g)
        finish_rows(g)
        if steps:
            @pl.when(g + AHEAD < chunks)
            def _():
                exchange(0, g + AHEAD)

        @pl.when(both(g % nk == 0, g > 0))
        def _():
            each(0, nr, lambda j: join((g // nk - 1) * nr + j))

        return carry

    def each(first, last, act):
        def go(c, carry):
            act(c)
            return carry

        lax.fori_loop(first, last, go, 0)

    lax.fori_loop(0, chunks, main, 0)
    each(0, early, enter)
    each(early, strips, join)
    each(0, early, finish_cols)
    for copy in fetches[4:]:
        copy.wait()

    def turn(n):
        turns = nr // pair
        return early + pair * (n % turns) + (core + n // turns) % pair

    @pl.when(z < nz - 1)
    def _():
        each(0, nr, lambda n: enter(turn(n)))

    def last(n):
        c = turn(n)

        @pl.when(z == nz - 1)
        def _():
            enter(c)

        finish_cols(c)
        per = GROUP // BLOCK
        each((c - early) * per, (c - early + 1) * per, mlp)

    each(0, nr, last)

    for s in range(steps):
        @pl.when(later(s))
        def _():
            each(0, chunks * PIECES, lambda n: vcopy(s, n // PIECES, n % PIECES).wait_send())

    def drain(c):
        @pl.when(both(owner(c), z < nz - 1))
        def _():
            for i in range(PIECES):
                chain_copy(c, i).wait_send()

        if pair == 2:
            @pl.when(jnp.logical_not(owner(c)))
            def _():
                join_copy(c).wait_send()

            @pl.when(both(owner(c), col != 1))
            def _():
                forward_copy(hin, c).wait_send()

    each(0, strips, drain)


def row_steps(nrow):
    steps = nrow.bit_length() - 1
    assert nrow == 1 << steps
    return steps


def pair_of(ncol):
    return 2 if ncol % 2 == 0 else 1


def emit(src, dst, sem):
    copy = pltpu.make_async_copy(src, dst, sem.at[0])
    copy.start()
    copy.wait()


def on_device(nrow, ncol, image, vert_rate, vert_coef, horiz_rate, horiz_coef, w_in, w_out):
    rows, cols, channels = image.shape
    modes = vert_rate.shape[0]
    halves = channels // LANES
    chunks, strips = halves * (cols // GROUP), halves * (rows // GROUP)
    steps = max(row_steps(nrow), 1)
    f32 = jnp.float32
    args = (image, vert_rate, vert_coef, horiz_rate, horiz_coef, w_in, w_out)
    half = pl.pallas_call(
        functools.partial(layer_kernel, nrow, ncol, rows, cols, modes, halves),
        out_shape=pltpu.VMEM((rows * cols, channels), jnp.bfloat16),
        in_specs=[pl.BlockSpec(memory_space=pltpu.MemorySpace.HBM)] * len(args),
        out_specs=pl.BlockSpec(memory_space=pltpu.MemorySpace.VMEM),
        scratch_shapes=[pltpu.VMEM(a.shape, a.dtype) for a in args] + [
            pltpu.VMEM((halves * rows * (cols + 1), LANES), f32),
            pltpu.VMEM((2, halves, modes, LANES), f32),
            pltpu.VMEM((2, halves, modes, LANES), f32),
            pltpu.VMEM((steps, halves, modes, LANES), f32),
            pltpu.VMEM((steps, halves, modes, LANES), f32),
            pltpu.VMEM((2, halves, modes, LANES), f32),
            pltpu.VMEM((2, halves, max(rows, cols) * modes, LANES), f32),
            pltpu.VMEM((steps, chunks, modes, GROUP, LANES), f32),
            pltpu.VMEM((steps, chunks, modes, GROUP, LANES), f32),
            pltpu.VMEM((chunks, modes, GROUP, LANES), f32),
        ] + [pltpu.VMEM((strips, modes, GROUP, LANES), f32)] * 5 + [
            pltpu.SemaphoreType.DMA((steps, chunks * PIECES)),
            pltpu.SemaphoreType.DMA((steps, chunks * PIECES)),
            pltpu.SemaphoreType.DMA((strips,)),
            pltpu.SemaphoreType.DMA((strips,)),
            pltpu.SemaphoreType.DMA((strips * PIECES,)),
            pltpu.SemaphoreType.DMA((strips * PIECES,)),
            pltpu.SemaphoreType.DMA((strips,)),
            pltpu.SemaphoreType.DMA((strips,)),
            pltpu.SemaphoreType.DMA((cols // GROUP,)),
            pltpu.SemaphoreType.DMA((6,)),
        ],
        compiler_params=pltpu.CompilerParams(collective_id=0, has_side_effects=True, vmem_limit_bytes=67043328 - rows * cols * channels * 2 - 4096),
    )(*args)
    full = pl.pallas_call(
        emit, out_shape=jax.ShapeDtypeStruct((rows * cols, channels), jnp.bfloat16),
        in_specs=[pl.BlockSpec(memory_space=pltpu.MemorySpace.VMEM)],
        out_specs=pl.BlockSpec(memory_space=pltpu.MemorySpace.HBM),
        scratch_shapes=[pltpu.SemaphoreType.DMA((1,))],
        compiler_params=pltpu.CompilerParams(vmem_limit_bytes=1000000),
    )(half)
    return full.reshape(rows, cols, channels)


def solution(mesh):
    placed = (P("row", "col", None), P(), P(), P(), P(), P(), P())
    return jax.shard_map(
        functools.partial(on_device, mesh.shape["row"], mesh.shape["col"]),
        mesh=mesh, in_specs=placed, out_specs=P("row", "col", None), check_vma=False,
    )
```

```python
import functools

import jax
import jax.numpy as jnp
from jax import lax
from jax.experimental import pallas as pl
from jax.experimental.pallas import tpu as pltpu
from jax.sharding import PartitionSpec as P

LANES = 128
GROUP = 16
BLOCK = 16
AHEAD = 2
PIECES = 1
HOPS = 1
MESH = pl.DeviceIdType.MESH
C0 = 0.7978845608028654
C1 = 0.7978845608028654 * 0.044715


def twice_gelu(x):
    return x + x * jnp.tanh(x * (C0 + C1 * (x * x)))


def layer_kernel(
    nrow, ncol, rows, cols, modes, halves,
    image_hbm, vrate_hbm, vcoef_hbm, hrate_hbm, hcoef_hbm, w_in_hbm, w_out_hbm, half,
    img, vrate, vcoef, hrate, hcoef, w_in, w_out, out,
    ptab, qtab, vdt, vdp, hdt, lead, vtot, vin, vpre, hin, hedge, hpart, hsum, hfwd, hcar,
    vsend, vrecv, asend, arecv, csend, crecv, fsend, frecv, img_sem, arg_sem,
):
    row = lax.axis_index("row")
    col = lax.axis_index("col")
    nk = cols // GROUP
    nr = rows // GROUP
    pitch = cols + 1
    size = rows * pitch
    steps = log_two(nrow)
    pair = pair_of(ncol)
    core, z, nz = col % pair, col // pair, ncol // pair
    chunks = halves * nk
    strips = halves * nr
    early = (halves - 1) * nr
    both = jnp.logical_and

    def bit_of(s):
        return (row // (1 << s)) % 2

    def row_partner(s):
        return row + (1 << s) * (1 - 2 * bit_of(s))

    def later(s):
        return row // (1 << s) != (nrow >> s) - 1

    barrier = pltpu.get_barrier_semaphore()
    always = row >= 0
    neighbours = [(always, {"row": row_partner(s)}) for s in range(steps)]
    if pair == 2:
        neighbours.append((always, {"col": col + 1 - 2 * core}))
    if nz > 1:
        neighbours.append((z > 0, {"col": col - pair}))
        neighbours.append((z < nz - 1, {"col": col + pair}))
    for there, device in neighbours:
        @pl.when(there)
        def _():
            pl.semaphore_signal(barrier, inc=1, device_id=device, device_id_type=MESH)

    def fetch_image(k):
        part = pl.ds(pl.multiple_of(k * GROUP, GROUP), GROUP)
        return pltpu.make_async_copy(image_hbm.at[:, part, :], img.at[:, part, :], img_sem.at[k])

    fetches = [
        pltpu.make_async_copy(src, dst, arg_sem.at[i])
        for i, (src, dst) in enumerate((
            (vrate_hbm, vrate), (vcoef_hbm, vcoef), (hrate_hbm, hrate), (hcoef_hbm, hcoef),
            (w_in_hbm, w_in), (w_out_hbm, w_out),
        ))
    ]
    for copy in fetches[:4]:
        copy.start()
    for k in range(nk):
        fetch_image(k).start()

    for copy in fetches[:4]:
        copy.wait()

    for axis, (rate, coef) in enumerate(((vrate, vcoef), (hrate, hcoef))):
        for h in range(halves):
            r = rate[:, h * LANES:(h + 1) * LANES]
            gain = jnp.sqrt(1.0 - jnp.exp(-2.0 * r))
            ptab[axis, h] = jnp.exp(-r)
            qtab[axis, h] = coef[:, h * LANES:(h + 1) * LANES] * gain

    for h in range(halves):
        r = vrate[:, h * LANES:(h + 1) * LANES]
        for s in range(steps):
            vdt[s, h] = jnp.exp(-r * (rows << s))
            vdp[s, h] = jnp.exp(-r * (rows * (row % (1 << s))).astype(jnp.float32))
        r = hrate[:, h * LANES:(h + 1) * LANES]
        hdt[0, h] = jnp.exp(-r * cols)
        hdt[1, h] = jnp.exp(-r * (cols * pair))

    def fill_lead():
        for axis, (rate, length) in enumerate(((vrate, rows), (hrate, cols))):

            def fill(i, carry):
                for h in range(halves):
                    r = rate[:, h * LANES:(h + 1) * LANES]
                    q = qtab[axis, h]
                    for j in range(modes):
                        t = i * modes + j
                        power = jnp.exp(-r * (t + 1).astype(jnp.float32))
                        lead[axis, h, pl.ds(pl.multiple_of(t * modes, modes), modes), :] = q * power
                return carry

            lax.fori_loop(0, length // modes, fill, 0)

    def spread(tab, axis, h):
        block = tab[axis, h]
        return [jnp.broadcast_to(block[m:m + 1, :], (GROUP, LANES)) for m in range(modes)]

    def total(terms):
        while len(terms) > 1:
            terms = [a + b for a, b in zip(terms[::2], terms[1::2])] + terms[len(terms) & ~1:]
        return terms[0]

    def span(i):
        return range(i * (modes // PIECES), (i + 1) * (modes // PIECES))

    def vcopy(s, g, i):
        part = pl.ds(i * (modes // PIECES), modes // PIECES)
        return pltpu.make_async_remote_copy(
            src_ref=vtot.at[s, g, part], dst_ref=vin.at[s, g, part],
            send_sem=vsend.at[s, g * PIECES + i], recv_sem=vrecv.at[s, g * PIECES + i],
            device_id={"row": row_partner(s)}, device_id_type=MESH,
        )

    def join_copy(c):
        return pltpu.make_async_remote_copy(
            src_ref=hedge.at[c], dst_ref=hpart.at[c], send_sem=asend.at[c], recv_sem=arecv.at[c],
            device_id={"col": col + 1 - 2 * core}, device_id_type=MESH,
        )

    def hop_copy(c, i):
        part = pl.ds(i * (modes // HOPS), modes // HOPS)
        return pltpu.make_async_remote_copy(
            src_ref=hsum.at[c, part], dst_ref=hin.at[c, part],
            send_sem=csend.at[c * HOPS + i], recv_sem=crecv.at[c * HOPS + i],
            device_id={"col": col + pair}, device_id_type=MESH,
        )

    def forward_copy(src, c):
        return pltpu.make_async_remote_copy(
            src_ref=src.at[c], dst_ref=hfwd.at[c], send_sem=fsend.at[c], recv_sem=frecv.at[c],
            device_id={"col": col + 1 - 2 * core}, device_id_type=MESH,
        )

    def owner(c):
        return c % pair == core

    def local(g):
        h, k = g // nk, g % nk

        @pl.when(h == 0)
        def _():
            fetch_image(k).wait()

        @pl.when(g == nk)
        def _():
            for copy in fetches[4:]:
                copy.start()

        p, q = spread(ptab, 0, h), spread(qtab, 0, h)
        lane = pl.multiple_of(h * LANES, LANES)
        first = pl.multiple_of(k * GROUP, GROUP)

        def step(t, state):
            u = img[t, pl.ds(first, GROUP), pl.ds(lane, LANES)].astype(jnp.float32)
            state = tuple(p[m] * state[m] + u for m in range(modes))
            y = total([q[m] * state[m] for m in range(modes)])
            out[pl.ds(h * size + t * pitch + first, GROUP), :] = y
            return state

        zero = jnp.zeros((GROUP, LANES), jnp.float32)
        state = lax.fori_loop(0, rows, step, (zero,) * modes, unroll=16)
        for m in range(modes):
            vtot[0, g, m] = state[m]

    def decay(tab, s, h, m):
        return jnp.broadcast_to(tab[s, h][m:m + 1, :], (GROUP, LANES))

    def exchange(s, g):
        h = g // nk
        bit = bit_of(s)
        onward = later(s + 1)
        for i in range(PIECES):
            @pl.when(jnp.logical_or(bit == 1, onward))
            def _():
                vcopy(s, g, i).wait_recv()

            if s + 1 < steps:
                @pl.when(onward)
                def _():
                    for m in span(i):
                        mine, theirs = vtot[s, g, m], vin[s, g, m]
                        older = jnp.where(bit == 0, mine, theirs)
                        newer = jnp.where(bit == 0, theirs, mine)
                        vtot[s + 1, g, m] = decay(vdt, s, h, m) * older + newer
                    vcopy(s + 1, g, i).start()

            @pl.when(bit == 1)
            def _():
                for m in span(i):
                    vpre[g, m] = decay(vdp, s, h, m) * vin[s, g, m] + vpre[g, m]

    def finish_rows(g):
        h, k = g // nk, g % nk
        first = pl.multiple_of(k * GROUP, GROUP)
        carried = [vpre[g, m] for m in range(modes)]

        def correct(t, carry):
            at = pl.ds(h * size + t * pitch + first, GROUP)
            here = lead[0, h, pl.ds(pl.multiple_of(t * modes, modes), modes), :]
            y = out[at, :] + total([here[m:m + 1, :] * carried[m] for m in range(modes)])
            act = (0.5 * twice_gelu(y)).astype(jnp.bfloat16)
            out[at, :] = act.astype(jnp.float32)
            return carry

        lax.fori_loop(0, rows, correct, 0, unroll=16)
        p, q = spread(ptab, 1, h), spread(qtab, 1, h)

        def group(j, carry):
            c = h * nr + j
            base = h * size + j * (GROUP * pitch) + first

            def step(t, state):
                at = pl.ds(base + t, GROUP, stride=pitch)
                u = out[at, :]
                state = tuple(p[m] * state[m] + u for m in range(modes))
                out[at, :] = total([q[m] * state[m] for m in range(modes)])
                return state

            state = lax.fori_loop(0, GROUP, step, tuple(hedge[c, m] for m in range(modes)), unroll=16)
            for m in range(modes):
                hedge[c, m] = state[m]

            if pair == 2:
                @pl.when(both(k == nk - 1, jnp.logical_not(owner(c))))
                def _():
                    join_copy(c).start()

            return carry

        lax.fori_loop(0, nr, group, 0)

    def join(c):
        h = c // nr

        @pl.when(owner(c))
        def _():
            if pair == 2:
                join_copy(c).wait_recv()
            for m in range(modes):
                mine = hedge[c, m]
                if pair == 2:
                    theirs = hpart[c, m]
                    older = jnp.where(core == 0, mine, theirs)
                    newer = jnp.where(core == 0, theirs, mine)
                    mine = decay(hdt, 0, h, m) * older + newer
                hsum[c, m] = mine
            if nz > 1:
                @pl.when(z == 0)
                def _():
                    for i in range(HOPS):
                        hop_copy(c, i).start()
            if pair == 2:
                @pl.when(col == 0)
                def _():
                    forward_copy(hedge, c).start()

    def enter(c):
        h = c // nr

        @pl.when(both(owner(c), z > 0))
        def _():
            for i in range(HOPS):
                part = range(i * (modes // HOPS), (i + 1) * (modes // HOPS))
                hop_copy(c, i).wait_recv()

                @pl.when(z < nz - 1)
                def _():
                    for m in part:
                        hsum[c, m] = decay(hdt, 1, h, m) * hin[c, m] + hsum[c, m]
                    hop_copy(c, i).start()

            if pair == 2:
                @pl.when(core == 0)
                def _():
                    for m in range(modes):
                        hpart[c, m] = decay(hdt, 0, h, m) * hin[c, m] + hedge[c, m]
                    forward_copy(hpart, c).start()
                    for m in range(modes):
                        hcar[c, m] = hin[c, m]

                @pl.when(core == 1)
                def _():
                    forward_copy(hin, c).start()
                    for m in range(modes):
                        hcar[c, m] = decay(hdt, 0, h, m) * hin[c, m] + hpart[c, m]
            else:
                for m in range(modes):
                    hcar[c, m] = hin[c, m]

        if pair == 2:
            @pl.when(both(owner(c), col == 1))
            def _():
                for m in range(modes):
                    hcar[c, m] = hpart[c, m]

            @pl.when(both(jnp.logical_not(owner(c)), col > 0))
            def _():
                forward_copy(hin, c).wait_recv()
                for m in range(modes):
                    hcar[c, m] = hfwd[c, m]

    def finish_cols(c):
        h, j = c // nr, c % nr

        @pl.when(col > 0)
        def _():
            carried = [hcar[c, m] for m in range(modes)]
            base = h * size + j * (GROUP * pitch)

            def correct(t, carry):
                at = pl.ds(base + t, GROUP, stride=pitch)
                here = lead[1, h, pl.ds(pl.multiple_of(t * modes, modes), modes), :]
                out[at, :] = out[at, :] + total([here[m:m + 1, :] * carried[m] for m in range(modes)])
                return carry

            lax.fori_loop(0, cols, correct, 0, unroll=16)

    def mlp(i):
        line = jnp.concatenate(
            [
                jnp.concatenate([out[pl.ds(h * size + (i * BLOCK + r) * pitch, cols), :] for h in range(halves)], axis=1)
                for r in range(BLOCK)
            ],
            axis=0,
        )
        scale = lax.rsqrt(jnp.mean(line * line, axis=-1, keepdims=True) + 1e-06)
        normed = (line * scale).astype(jnp.bfloat16)
        pre = jnp.dot(normed, w_in[...], preferred_element_type=jnp.float32).astype(jnp.bfloat16)
        hidden = twice_gelu(pre)
        result = line + 0.5 * jnp.dot(hidden, w_out[...], preferred_element_type=jnp.float32)
        half[pl.ds(pl.multiple_of(i * (BLOCK * cols), BLOCK * cols), BLOCK * cols), :] = result.astype(half.dtype)

    hedge[...] = jnp.zeros_like(hedge)
    vpre[...] = jnp.zeros_like(vpre)

    def scan(s, carry):
        local(s)

        @pl.when(s == 0)
        def _():
            pl.semaphore_wait(barrier, sum(jnp.where(there, 1, 0) for there, _ in neighbours))

        if steps:
            @pl.when(later(0))
            def _():
                for i in range(PIECES):
                    vcopy(0, s, i).start()

            @pl.when(s >= chunks - AHEAD)
            def _():
                exchange(0, s - (chunks - AHEAD))

        return carry

    lax.fori_loop(0, chunks, scan, 0)
    fill_lead()

    def main(g, carry):
        for s in range(1, steps):
            exchange(s, g)
        finish_rows(g)
        if steps:
            @pl.when(g + AHEAD < chunks)
            def _():
                exchange(0, g + AHEAD)

        @pl.when(both(g % nk == 0, g > 0))
        def _():
            each(0, nr, lambda j: join((g // nk - 1) * nr + j))

        return carry

    def each(first, last, act):
        def go(c, carry):
            act(c)
            return carry

        lax.fori_loop(first, last, go, 0)

    lax.fori_loop(0, chunks, main, 0)

    def turn(n):
        turns = nr // pair
        return (n // nr) * nr + pair * (n % turns) + (core + (n % nr) // turns) % pair

    each(0, early, lambda n: enter(turn(n)))
    each(early, strips, lambda n: join(turn(n)))
    each(0, early, lambda n: finish_cols(turn(n)))
    for copy in fetches[4:]:
        copy.wait()

    @pl.when(z < nz - 1)
    def _():
        each(early, strips, lambda n: enter(turn(n)))

    def last(n):
        c = turn(n)

        @pl.when(z == nz - 1)
        def _():
            enter(c)

        finish_cols(c)
        per = GROUP // BLOCK
        each((c - early) * per, (c - early + 1) * per, mlp)

    each(early, strips, last)

    for s in range(steps):
        @pl.when(later(s))
        def _():
            each(0, chunks * PIECES, lambda n: vcopy(s, n // PIECES, n % PIECES).wait_send())

    def drain(c):
        if nz > 1:
            @pl.when(both(owner(c), z < nz - 1))
            def _():
                for i in range(HOPS):
                    hop_copy(c, i).wait_send()

        if pair == 2:
            @pl.when(jnp.logical_not(owner(c)))
            def _():
                join_copy(c).wait_send()

            @pl.when(both(owner(c), col != 1))
            def _():
                forward_copy(hin, c).wait_send()

    each(0, strips, drain)


def log_two(count):
    steps = count.bit_length() - 1
    assert count == 1 << steps
    return steps


def pair_of(ncol):
    return 2 if ncol % 2 == 0 else 1


def emit(src, dst, sem):
    copy = pltpu.make_async_copy(src, dst, sem.at[0])
    copy.start()
    copy.wait()


def on_device(nrow, ncol, image, vert_rate, vert_coef, horiz_rate, horiz_coef, w_in, w_out):
    rows, cols, channels = image.shape
    modes = vert_rate.shape[0]
    halves = channels // LANES
    chunks, strips = halves * (cols // GROUP), halves * (rows // GROUP)
    steps = max(log_two(nrow), 1)
    f32 = jnp.float32
    args = (image, vert_rate, vert_coef, horiz_rate, horiz_coef, w_in, w_out)
    half = pl.pallas_call(
        functools.partial(layer_kernel, nrow, ncol, rows, cols, modes, halves),
        out_shape=pltpu.VMEM((rows * cols, channels), jnp.bfloat16),
        in_specs=[pl.BlockSpec(memory_space=pltpu.MemorySpace.HBM)] * len(args),
        out_specs=pl.BlockSpec(memory_space=pltpu.MemorySpace.VMEM),
        scratch_shapes=[pltpu.VMEM(a.shape, a.dtype) for a in args] + [
            pltpu.VMEM((halves * rows * (cols + 1), LANES), f32),
            pltpu.VMEM((2, halves, modes, LANES), f32),
            pltpu.VMEM((2, halves, modes, LANES), f32),
            pltpu.VMEM((steps, halves, modes, LANES), f32),
            pltpu.VMEM((steps, halves, modes, LANES), f32),
            pltpu.VMEM((2, halves, modes, LANES), f32),
            pltpu.VMEM((2, halves, max(rows, cols) * modes, LANES), f32),
            pltpu.VMEM((steps, chunks, modes, GROUP, LANES), f32),
            pltpu.VMEM((steps, chunks, modes, GROUP, LANES), f32),
            pltpu.VMEM((chunks, modes, GROUP, LANES), f32),
        ] + [pltpu.VMEM((strips, modes, GROUP, LANES), f32)] * 6 + [
            pltpu.SemaphoreType.DMA((steps, chunks * PIECES)),
            pltpu.SemaphoreType.DMA((steps, chunks * PIECES)),
            pltpu.SemaphoreType.DMA((strips,)),
            pltpu.SemaphoreType.DMA((strips,)),
            pltpu.SemaphoreType.DMA((strips * HOPS,)),
            pltpu.SemaphoreType.DMA((strips * HOPS,)),
            pltpu.SemaphoreType.DMA((strips,)),
            pltpu.SemaphoreType.DMA((strips,)),
            pltpu.SemaphoreType.DMA((cols // GROUP,)),
            pltpu.SemaphoreType.DMA((6,)),
        ],
        compiler_params=pltpu.CompilerParams(collective_id=0, has_side_effects=True, vmem_limit_bytes=67043328 - rows * cols * channels * 2 - 4096),
    )(*args)
    full = pl.pallas_call(
        emit, out_shape=jax.ShapeDtypeStruct((rows * cols, channels), jnp.bfloat16),
        in_specs=[pl.BlockSpec(memory_space=pltpu.MemorySpace.VMEM)],
        out_specs=pl.BlockSpec(memory_space=pltpu.MemorySpace.HBM),
        scratch_shapes=[pltpu.SemaphoreType.DMA((1,))],
        compiler_params=pltpu.CompilerParams(vmem_limit_bytes=1000000),
    )(half)
    return full.reshape(rows, cols, channels)


def solution(mesh):
    placed = (P("row", "col", None), P(), P(), P(), P(), P(), P())
    return jax.shard_map(
        functools.partial(on_device, mesh.shape["row"], mesh.shape["col"]),
        mesh=mesh, in_specs=placed, out_specs=P("row", "col", None), check_vma=False,
    )
```

```python
import functools

import jax
import jax.numpy as jnp
from jax import lax
from jax.experimental import pallas as pl
from jax.experimental.pallas import tpu as pltpu
from jax.sharding import PartitionSpec as P

LANES = 128
GROUP = 16
BLOCK = 16
AHEAD = 3
PIECES = 1
HOPS = 1
PARTS = 8
MESH = pl.DeviceIdType.MESH
C0 = 0.7978845608028654
C1 = 0.7978845608028654 * 0.044715


def twice_gelu(x):
    return x + x * jnp.tanh(x * (C0 + C1 * (x * x)))


def layer_kernel(
    nrow, ncol, rows, cols, modes, halves,
    image_hbm, vrate_hbm, vcoef_hbm, hrate_hbm, hcoef_hbm, w_in_hbm, w_out_hbm, half,
    img, vrate, vcoef, hrate, hcoef, w_in, w_out, out,
    ptab, qtab, vdt, vdp, hdt, lead, vtot, vin, vpre, hin, hedge, hpart, hsum, hfwd, hcar,
    vsend, vrecv, asend, arecv, csend, crecv, fsend, frecv, img_sem, arg_sem,
):
    row = lax.axis_index("row")
    col = lax.axis_index("col")
    nk = cols // GROUP
    nr = rows // GROUP
    pitch = cols + 1
    size = rows * pitch
    steps = log_two(nrow)
    pair = pair_of(ncol)
    core, z, nz = col % pair, col // pair, ncol // pair
    chunks = halves * nk
    strips = halves * nr
    early = (halves - 1) * nr
    both = jnp.logical_and

    def bit_of(s):
        return (row // (1 << s)) % 2

    def row_partner(s):
        return row + (1 << s) * (1 - 2 * bit_of(s))

    def later(s):
        return row // (1 << s) != (nrow >> s) - 1

    barrier = pltpu.get_barrier_semaphore()
    always = row >= 0
    neighbours = [(always, {"row": row_partner(s)}) for s in range(steps)]
    if pair == 2:
        neighbours.append((always, {"col": col + 1 - 2 * core}))
    if nz > 1:
        neighbours.append((z > 0, {"col": col - pair}))
        neighbours.append((z < nz - 1, {"col": col + pair}))
    for there, device in neighbours:
        @pl.when(there)
        def _():
            pl.semaphore_signal(barrier, inc=1, device_id=device, device_id_type=MESH)

    def fetch_image(k):
        part = pl.ds(pl.multiple_of(k * GROUP, GROUP), GROUP)
        return pltpu.make_async_copy(image_hbm.at[:, part, :], img.at[:, part, :], img_sem.at[k])

    fetches = [
        pltpu.make_async_copy(src, dst, arg_sem.at[i])
        for i, (src, dst) in enumerate((
            (vrate_hbm, vrate), (vcoef_hbm, vcoef), (hrate_hbm, hrate), (hcoef_hbm, hcoef),
            (w_in_hbm, w_in), (w_out_hbm, w_out),
        ))
    ]
    for copy in fetches[:4]:
        copy.start()
    for k in range(nk):
        fetch_image(k).start()

    for copy in fetches[:4]:
        copy.wait()

    for axis, (rate, coef) in enumerate(((vrate, vcoef), (hrate, hcoef))):
        for h in range(halves):
            r = rate[:, h * LANES:(h + 1) * LANES]
            gain = jnp.sqrt(1.0 - jnp.exp(-2.0 * r))
            ptab[axis, h] = jnp.exp(-r)
            qtab[axis, h] = coef[:, h * LANES:(h + 1) * LANES] * (gain if axis == 0 else 0.5 * gain)

    for h in range(halves):
        r = vrate[:, h * LANES:(h + 1) * LANES]
        for s in range(steps):
            vdt[s, h] = jnp.exp(-r * (rows << s))
            vdp[s, h] = jnp.exp(-r * (rows * (row % (1 << s))).astype(jnp.float32))
        r = hrate[:, h * LANES:(h + 1) * LANES]
        hdt[0, h] = jnp.exp(-r * cols)
        hdt[1, h] = jnp.exp(-r * (cols * pair))

    def fill_lead():
        for axis, (rate, length) in enumerate(((vrate, rows), (hrate, cols))):

            def fill(i, carry):
                for h in range(halves):
                    r = rate[:, h * LANES:(h + 1) * LANES]
                    q = qtab[axis, h]
                    for j in range(modes):
                        t = i * modes + j
                        power = jnp.exp(-r * (t + 1).astype(jnp.float32))
                        lead[axis, h, pl.ds(pl.multiple_of(t * modes, modes), modes), :] = q * power
                return carry

            lax.fori_loop(0, length // modes, fill, 0)

    def spread(tab, axis, h):
        block = tab[axis, h]
        return [jnp.broadcast_to(block[m:m + 1, :], (GROUP, LANES)) for m in range(modes)]

    def total(terms):
        while len(terms) > 1:
            terms = [a + b for a, b in zip(terms[::2], terms[1::2])] + terms[len(terms) & ~1:]
        return terms[0]

    def span(i):
        return range(i * (modes // PIECES), (i + 1) * (modes // PIECES))

    def vcopy(s, g, i):
        part = pl.ds(i * (modes // PIECES), modes // PIECES)
        return pltpu.make_async_remote_copy(
            src_ref=vtot.at[s, g, part], dst_ref=vin.at[s, g, part],
            send_sem=vsend.at[s, g * PIECES + i], recv_sem=vrecv.at[s, g * PIECES + i],
            device_id={"row": row_partner(s)}, device_id_type=MESH,
        )

    def join_copy(c):
        return pltpu.make_async_remote_copy(
            src_ref=hedge.at[c], dst_ref=hpart.at[c], send_sem=asend.at[c], recv_sem=arecv.at[c],
            device_id={"col": col + 1 - 2 * core}, device_id_type=MESH,
        )

    def hop_copy(c, i):
        part = pl.ds(i * (modes // HOPS), modes // HOPS)
        return pltpu.make_async_remote_copy(
            src_ref=hsum.at[c, part], dst_ref=hin.at[c, part],
            send_sem=csend.at[c * HOPS + i], recv_sem=crecv.at[c * HOPS + i],
            device_id={"col": col + pair}, device_id_type=MESH,
        )

    def forward_copy(src, c):
        return pltpu.make_async_remote_copy(
            src_ref=src.at[c], dst_ref=hfwd.at[c], send_sem=fsend.at[c], recv_sem=frecv.at[c],
            device_id={"col": col + 1 - 2 * core}, device_id_type=MESH,
        )

    def owner(c):
        return c % pair == core

    def local(g):
        h, k = g // nk, g % nk

        @pl.when(h == 0)
        def _():
            fetch_image(k).wait()

        @pl.when(g == nk)
        def _():
            for copy in fetches[4:]:
                copy.start()

        p, q = spread(ptab, 0, h), spread(qtab, 0, h)
        lane = pl.multiple_of(h * LANES, LANES)
        first = pl.multiple_of(k * GROUP, GROUP)

        def step(t, state):
            u = img[t, pl.ds(first, GROUP), pl.ds(lane, LANES)].astype(jnp.float32)
            state = tuple(p[m] * state[m] + u for m in range(modes))
            y = total([q[m] * state[m] for m in range(modes)])
            out[pl.ds(h * size + t * pitch + first, GROUP), :] = y
            return state

        zero = jnp.zeros((GROUP, LANES), jnp.float32)
        state = lax.fori_loop(0, rows, step, (zero,) * modes, unroll=16)
        for m in range(modes):
            vtot[0, g, m] = state[m]

    def decay(tab, s, h, m):
        return jnp.broadcast_to(tab[s, h][m:m + 1, :], (GROUP, LANES))

    def exchange(s, g):
        h = g // nk
        bit = bit_of(s)
        onward = later(s + 1)
        for i in range(PIECES):
            @pl.when(jnp.logical_or(bit == 1, onward))
            def _():
                vcopy(s, g, i).wait_recv()

            if s + 1 < steps:
                @pl.when(onward)
                def _():
                    for m in span(i):
                        mine, theirs = vtot[s, g, m], vin[s, g, m]
                        older = jnp.where(bit == 0, mine, theirs)
                        newer = jnp.where(bit == 0, theirs, mine)
                        vtot[s + 1, g, m] = decay(vdt, s, h, m) * older + newer
                    vcopy(s + 1, g, i).start()

            @pl.when(bit == 1)
            def _():
                for m in span(i):
                    vpre[g, m] = decay(vdp, s, h, m) * vin[s, g, m] + vpre[g, m]

    def finish_rows(g):
        h, k = g // nk, g % nk
        first = pl.multiple_of(k * GROUP, GROUP)
        carried = [vpre[g, m] for m in range(modes)]

        def correct(t, carry):
            at = pl.ds(h * size + t * pitch + first, GROUP)
            here = lead[0, h, pl.ds(pl.multiple_of(t * modes, modes), modes), :]
            y = out[at, :] + total([here[m:m + 1, :] * carried[m] for m in range(modes)])
            act = twice_gelu(y).astype(jnp.bfloat16)
            out[at, :] = act.astype(jnp.float32)
            return carry

        lax.fori_loop(0, rows, correct, 0, unroll=16)
        p, q = spread(ptab, 1, h), spread(qtab, 1, h)

        def group(j, carry):
            c = h * nr + j
            base = h * size + j * (GROUP * pitch) + first

            def step(t, state):
                at = pl.ds(base + t, GROUP, stride=pitch)
                u = out[at, :]
                state = tuple(p[m] * state[m] + u for m in range(modes))
                out[at, :] = total([q[m] * state[m] for m in range(modes)])
                return state

            state = lax.fori_loop(0, GROUP, step, tuple(hedge[c, m] for m in range(modes)), unroll=16)
            for m in range(modes):
                hedge[c, m] = state[m]

            if pair == 2:
                @pl.when(both(k == nk - 1, jnp.logical_not(owner(c))))
                def _():
                    join_copy(c).start()

            return carry

        lax.fori_loop(0, nr, group, 0)

    def join(c):
        h = c // nr

        @pl.when(owner(c))
        def _():
            if pair == 2:
                join_copy(c).wait_recv()
            for m in range(modes):
                mine = hedge[c, m]
                if pair == 2:
                    theirs = hpart[c, m]
                    older = jnp.where(core == 0, mine, theirs)
                    newer = jnp.where(core == 0, theirs, mine)
                    mine = decay(hdt, 0, h, m) * older + newer
                hsum[c, m] = mine
            if nz > 1:
                @pl.when(z == 0)
                def _():
                    for i in range(HOPS):
                        hop_copy(c, i).start()
            if pair == 2:
                @pl.when(col == 0)
                def _():
                    forward_copy(hedge, c).start()

    def enter(c):
        h = c // nr

        @pl.when(both(owner(c), z > 0))
        def _():
            for i in range(HOPS):
                part = range(i * (modes // HOPS), (i + 1) * (modes // HOPS))
                hop_copy(c, i).wait_recv()

                @pl.when(z < nz - 1)
                def _():
                    for m in part:
                        hsum[c, m] = decay(hdt, 1, h, m) * hin[c, m] + hsum[c, m]
                    hop_copy(c, i).start()

            if pair == 2:
                @pl.when(core == 0)
                def _():
                    for m in range(modes):
                        hpart[c, m] = decay(hdt, 0, h, m) * hin[c, m] + hedge[c, m]
                    forward_copy(hpart, c).start()
                    for m in range(modes):
                        hcar[c, m] = hin[c, m]

                @pl.when(core == 1)
                def _():
                    forward_copy(hin, c).start()
                    for m in range(modes):
                        hcar[c, m] = decay(hdt, 0, h, m) * hin[c, m] + hpart[c, m]
            else:
                for m in range(modes):
                    hcar[c, m] = hin[c, m]

        if pair == 2:
            @pl.when(both(owner(c), col == 1))
            def _():
                for m in range(modes):
                    hcar[c, m] = hpart[c, m]

            @pl.when(both(jnp.logical_not(owner(c)), col > 0))
            def _():
                forward_copy(hin, c).wait_recv()
                for m in range(modes):
                    hcar[c, m] = hfwd[c, m]

    def finish_cols(c):
        h, j = c // nr, c % nr

        @pl.when(col > 0)
        def _():
            carried = [hcar[c, m] for m in range(modes)]
            base = h * size + j * (GROUP * pitch)

            def correct(t, carry):
                at = pl.ds(base + t, GROUP, stride=pitch)
                here = lead[1, h, pl.ds(pl.multiple_of(t * modes, modes), modes), :]
                out[at, :] = out[at, :] + total([here[m:m + 1, :] * carried[m] for m in range(modes)])
                return carry

            lax.fori_loop(0, cols, correct, 0, unroll=16)

    def mlp(i):
        line = jnp.concatenate(
            [
                jnp.concatenate([out[pl.ds(h * size + (i * BLOCK + r) * pitch, cols), :] for h in range(halves)], axis=1)
                for r in range(BLOCK)
            ],
            axis=0,
        )
        scale = lax.rsqrt(jnp.mean(line * line, axis=-1, keepdims=True) + 1e-06)
        normed = (line * scale).astype(jnp.bfloat16)
        pre = jnp.dot(normed, w_in[...], preferred_element_type=jnp.float32).astype(jnp.bfloat16)
        hidden = twice_gelu(pre)
        result = line + 0.5 * jnp.dot(hidden, w_out[...], preferred_element_type=jnp.float32)
        half[pl.ds(pl.multiple_of(i * (BLOCK * cols), BLOCK * cols), BLOCK * cols), :] = result.astype(half.dtype)

    hedge[...] = jnp.zeros_like(hedge)
    vpre[...] = jnp.zeros_like(vpre)

    def scan(s, carry):
        local(s)

        @pl.when(s == 0)
        def _():
            pl.semaphore_wait(barrier, sum(jnp.where(there, 1, 0) for there, _ in neighbours))

        if steps:
            @pl.when(later(0))
            def _():
                for i in range(PIECES):
                    vcopy(0, s, i).start()

            @pl.when(s >= chunks - AHEAD)
            def _():
                exchange(0, s - (chunks - AHEAD))

        return carry

    lax.fori_loop(0, chunks, scan, 0)
    fill_lead()

    def main(g, carry):
        for s in range(1, steps):
            exchange(s, g)
        finish_rows(g)
        if steps:
            @pl.when(g + AHEAD < chunks)
            def _():
                exchange(0, g + AHEAD)

        @pl.when(both(g % nk == 0, g > 0))
        def _():
            each(0, nr, lambda j: join((g // nk - 1) * nr + j))

        return carry

    def each(first, last, act):
        def go(c, carry):
            act(c)
            return carry

        lax.fori_loop(first, last, go, 0)

    lax.fori_loop(0, chunks, main, 0)

    def turn(n):
        turns = nr // pair
        return (n // nr) * nr + pair * (n % turns) + (core + (n % nr) // turns) % pair

    each(0, early, lambda n: enter(turn(n)))
    each(early, strips, lambda n: join(turn(n)))
    each(0, early, lambda n: finish_cols(turn(n)))
    for copy in fetches[4:]:
        copy.wait()

    @pl.when(z < nz - 1)
    def _():
        each(early, strips, lambda n: enter(turn(n)))

    def last(n):
        c = turn(n)

        @pl.when(z == nz - 1)
        def _():
            enter(c)

        finish_cols(c)
        per = GROUP // BLOCK
        each((c - early) * per, (c - early + 1) * per, mlp)

    each(early, strips, last)

    for s in range(steps):
        @pl.when(later(s))
        def _():
            each(0, chunks * PIECES, lambda n: vcopy(s, n // PIECES, n % PIECES).wait_send())

    def drain(c):
        if nz > 1:
            @pl.when(both(owner(c), z < nz - 1))
            def _():
                for i in range(HOPS):
                    hop_copy(c, i).wait_send()

        if pair == 2:
            @pl.when(jnp.logical_not(owner(c)))
            def _():
                join_copy(c).wait_send()

            @pl.when(both(owner(c), col != 1))
            def _():
                forward_copy(hin, c).wait_send()

    each(0, strips, drain)


def log_two(count):
    steps = count.bit_length() - 1
    assert count == 1 << steps
    return steps


def pair_of(ncol):
    return 2 if ncol % 2 == 0 else 1


def emit(src, dst, sem):
    rows = src.shape[0] // PARTS
    copies = [
        pltpu.make_async_copy(src.at[pl.ds(i * rows, rows)], dst.at[pl.ds(i * rows, rows)], sem.at[i])
        for i in range(PARTS)
    ]
    for copy in copies:
        copy.start()
    for copy in copies:
        copy.wait()


def on_device(nrow, ncol, image, vert_rate, vert_coef, horiz_rate, horiz_coef, w_in, w_out):
    rows, cols, channels = image.shape
    modes = vert_rate.shape[0]
    halves = channels // LANES
    chunks, strips = halves * (cols // GROUP), halves * (rows // GROUP)
    steps = max(log_two(nrow), 1)
    f32 = jnp.float32
    args = (image, vert_rate, vert_coef, horiz_rate, horiz_coef, w_in, w_out)
    half = pl.pallas_call(
        functools.partial(layer_kernel, nrow, ncol, rows, cols, modes, halves),
        out_shape=pltpu.VMEM((rows * cols, channels), jnp.bfloat16),
        in_specs=[pl.BlockSpec(memory_space=pltpu.MemorySpace.HBM)] * len(args),
        out_specs=pl.BlockSpec(memory_space=pltpu.MemorySpace.VMEM),
        scratch_shapes=[pltpu.VMEM(a.shape, a.dtype) for a in args] + [
            pltpu.VMEM((halves * rows * (cols + 1), LANES), f32),
            pltpu.VMEM((2, halves, modes, LANES), f32),
            pltpu.VMEM((2, halves, modes, LANES), f32),
            pltpu.VMEM((steps, halves, modes, LANES), f32),
            pltpu.VMEM((steps, halves, modes, LANES), f32),
            pltpu.VMEM((2, halves, modes, LANES), f32),
            pltpu.VMEM((2, halves, max(rows, cols) * modes, LANES), f32),
            pltpu.VMEM((steps, chunks, modes, GROUP, LANES), f32),
            pltpu.VMEM((steps, chunks, modes, GROUP, LANES), f32),
            pltpu.VMEM((chunks, modes, GROUP, LANES), f32),
        ] + [pltpu.VMEM((strips, modes, GROUP, LANES), f32)] * 6 + [
            pltpu.SemaphoreType.DMA((steps, chunks * PIECES)),
            pltpu.SemaphoreType.DMA((steps, chunks * PIECES)),
            pltpu.SemaphoreType.DMA((strips,)),
            pltpu.SemaphoreType.DMA((strips,)),
            pltpu.SemaphoreType.DMA((strips * HOPS,)),
            pltpu.SemaphoreType.DMA((strips * HOPS,)),
            pltpu.SemaphoreType.DMA((strips,)),
            pltpu.SemaphoreType.DMA((strips,)),
            pltpu.SemaphoreType.DMA((cols // GROUP,)),
            pltpu.SemaphoreType.DMA((6,)),
        ],
        compiler_params=pltpu.CompilerParams(collective_id=0, has_side_effects=True, vmem_limit_bytes=67043328 - rows * cols * channels * 2 - 4096),
    )(*args)
    full = pl.pallas_call(
        emit, out_shape=jax.ShapeDtypeStruct((rows * cols, channels), jnp.bfloat16),
        in_specs=[pl.BlockSpec(memory_space=pltpu.MemorySpace.VMEM)],
        out_specs=pl.BlockSpec(memory_space=pltpu.MemorySpace.HBM),
        scratch_shapes=[pltpu.SemaphoreType.DMA((PARTS,))],
        compiler_params=pltpu.CompilerParams(vmem_limit_bytes=1000000),
    )(half)
    return full.reshape(rows, cols, channels)


def solution(mesh):
    placed = (P("row", "col", None), P(), P(), P(), P(), P(), P())
    return jax.shard_map(
        functools.partial(on_device, mesh.shape["row"], mesh.shape["col"]),
        mesh=mesh, in_specs=placed, out_specs=P("row", "col", None), check_vma=False,
    )
```

```python
import functools

import jax
import jax.numpy as jnp
from jax import lax
from jax.experimental import pallas as pl
from jax.experimental.pallas import tpu as pltpu
from jax.sharding import PartitionSpec as P

LANES = 128
GROUP = 16
BLOCK = 16
AHEAD = 3
PIECES = 1
HOPS = 1
PARTS = 8
MESH = pl.DeviceIdType.MESH
C0 = 0.7978845608028654
C1 = 0.7978845608028654 * 0.044715


def twice_gelu(x):
    return x + x * jnp.tanh(x * (C0 + C1 * (x * x)))


def layer_kernel(
    nrow, ncol, rows, cols, modes, halves,
    image_hbm, vrate_hbm, vcoef_hbm, hrate_hbm, hcoef_hbm, w_in_hbm, w_out_hbm, half,
    img, vrate, vcoef, hrate, hcoef, w_in, w_out, out,
    ptab, qtab, vdt, vdp, hdt, lead, vtot, vin, vpre, hin, hedge, hpart, hsum, hfwd, hcar,
    vsend, vrecv, asend, arecv, csend, crecv, fsend, frecv, img_sem, arg_sem,
):
    row = lax.axis_index("row")
    col = lax.axis_index("col")
    nk = cols // GROUP
    nr = rows // GROUP
    pitch = cols + 1
    size = rows * pitch
    steps = log_two(nrow)
    pair = pair_of(ncol)
    core, z, nz = col % pair, col // pair, ncol // pair
    chunks = halves * nk
    strips = halves * nr
    early = (halves - 1) * nr
    both = jnp.logical_and

    def bit_of(s):
        return (row // (1 << s)) % 2

    def row_partner(s):
        return row + (1 << s) * (1 - 2 * bit_of(s))

    def later(s):
        return row // (1 << s) != (nrow >> s) - 1

    barrier = pltpu.get_barrier_semaphore()
    always = row >= 0
    neighbours = [(always, {"row": row_partner(s)}) for s in range(steps)]
    if pair == 2:
        neighbours.append((always, {"col": col + 1 - 2 * core}))
    if nz > 1:
        neighbours.append((z > 0, {"col": col - pair}))
        neighbours.append((z < nz - 1, {"col": col + pair}))
    for there, device in neighbours:
        @pl.when(there)
        def _():
            pl.semaphore_signal(barrier, inc=1, device_id=device, device_id_type=MESH)

    def fetch_image(g):
        part = pl.ds(pl.multiple_of(g % nk * GROUP, GROUP), GROUP)
        lane = pl.ds(pl.multiple_of(g // nk * LANES, LANES), LANES)
        return pltpu.make_async_copy(image_hbm.at[:, part, lane], img.at[:, part, lane], img_sem.at[g])

    fetches = [
        pltpu.make_async_copy(src, dst, arg_sem.at[i])
        for i, (src, dst) in enumerate((
            (vrate_hbm, vrate), (vcoef_hbm, vcoef), (hrate_hbm, hrate), (hcoef_hbm, hcoef),
            (w_in_hbm, w_in), (w_out_hbm, w_out),
        ))
    ]
    for copy in fetches[:4]:
        copy.start()
    for g in range(chunks):
        fetch_image(g).start()

    for copy in fetches[:4]:
        copy.wait()

    for axis, (rate, coef) in enumerate(((vrate, vcoef), (hrate, hcoef))):
        for h in range(halves):
            r = rate[:, h * LANES:(h + 1) * LANES]
            gain = jnp.sqrt(1.0 - jnp.exp(-2.0 * r))
            ptab[axis, h] = jnp.exp(-r)
            qtab[axis, h] = coef[:, h * LANES:(h + 1) * LANES] * (gain if axis == 0 else 0.5 * gain)

    for h in range(halves):
        r = vrate[:, h * LANES:(h + 1) * LANES]
        for s in range(steps):
            vdt[s, h] = jnp.exp(-r * (rows << s))
            vdp[s, h] = jnp.exp(-r * (rows * (row % (1 << s))).astype(jnp.float32))
        r = hrate[:, h * LANES:(h + 1) * LANES]
        hdt[0, h] = jnp.exp(-r * cols)
        hdt[1, h] = jnp.exp(-r * (cols * pair))

    def fill_lead():
        for axis, (rate, length) in enumerate(((vrate, rows), (hrate, cols))):

            def fill(i, carry):
                for h in range(halves):
                    r = rate[:, h * LANES:(h + 1) * LANES]
                    q = qtab[axis, h]
                    for j in range(modes):
                        t = i * modes + j
                        power = jnp.exp(-r * (t + 1).astype(jnp.float32))
                        lead[axis, h, pl.ds(pl.multiple_of(t * modes, modes), modes), :] = q * power
                return carry

            lax.fori_loop(0, length // modes, fill, 0)

    def spread(tab, axis, h):
        block = tab[axis, h]
        return [jnp.broadcast_to(block[m:m + 1, :], (GROUP, LANES)) for m in range(modes)]

    def total(terms):
        while len(terms) > 1:
            terms = [a + b for a, b in zip(terms[::2], terms[1::2])] + terms[len(terms) & ~1:]
        return terms[0]

    def span(i):
        return range(i * (modes // PIECES), (i + 1) * (modes // PIECES))

    def vcopy(s, g, i):
        part = pl.ds(i * (modes // PIECES), modes // PIECES)
        return pltpu.make_async_remote_copy(
            src_ref=vtot.at[s, g, part], dst_ref=vin.at[s, g, part],
            send_sem=vsend.at[s, g * PIECES + i], recv_sem=vrecv.at[s, g * PIECES + i],
            device_id={"row": row_partner(s)}, device_id_type=MESH,
        )

    def join_copy(c):
        return pltpu.make_async_remote_copy(
            src_ref=hedge.at[c], dst_ref=hpart.at[c], send_sem=asend.at[c], recv_sem=arecv.at[c],
            device_id={"col": col + 1 - 2 * core}, device_id_type=MESH,
        )

    def hop_copy(c, i):
        part = pl.ds(i * (modes // HOPS), modes // HOPS)
        return pltpu.make_async_remote_copy(
            src_ref=hsum.at[c, part], dst_ref=hin.at[c, part],
            send_sem=csend.at[c * HOPS + i], recv_sem=crecv.at[c * HOPS + i],
            device_id={"col": col + pair}, device_id_type=MESH,
        )

    def forward_copy(src, c):
        return pltpu.make_async_remote_copy(
            src_ref=src.at[c], dst_ref=hfwd.at[c], send_sem=fsend.at[c], recv_sem=frecv.at[c],
            device_id={"col": col + 1 - 2 * core}, device_id_type=MESH,
        )

    def owner(c):
        return c % pair == core

    def local(g):
        h, k = g // nk, g % nk

        fetch_image(g).wait()

        @pl.when(g == nk)
        def _():
            for copy in fetches[4:]:
                copy.start()

        p, q = spread(ptab, 0, h), spread(qtab, 0, h)
        lane = pl.multiple_of(h * LANES, LANES)
        first = pl.multiple_of(k * GROUP, GROUP)

        def step(t, state):
            u = img[t, pl.ds(first, GROUP), pl.ds(lane, LANES)].astype(jnp.float32)
            state = tuple(p[m] * state[m] + u for m in range(modes))
            y = total([q[m] * state[m] for m in range(modes)])
            out[pl.ds(h * size + t * pitch + first, GROUP), :] = y
            return state

        zero = jnp.zeros((GROUP, LANES), jnp.float32)
        state = lax.fori_loop(0, rows, step, (zero,) * modes, unroll=32)
        for m in range(modes):
            vtot[0, g, m] = state[m]

    def decay(tab, s, h, m):
        return jnp.broadcast_to(tab[s, h][m:m + 1, :], (GROUP, LANES))

    def exchange(s, g):
        h = g // nk
        bit = bit_of(s)
        onward = later(s + 1)
        for i in range(PIECES):
            @pl.when(jnp.logical_or(bit == 1, onward))
            def _():
                vcopy(s, g, i).wait_recv()

            if s + 1 < steps:
                @pl.when(onward)
                def _():
                    for m in span(i):
                        mine, theirs = vtot[s, g, m], vin[s, g, m]
                        older = jnp.where(bit == 0, mine, theirs)
                        newer = jnp.where(bit == 0, theirs, mine)
                        vtot[s + 1, g, m] = decay(vdt, s, h, m) * older + newer
                    vcopy(s + 1, g, i).start()

            @pl.when(bit == 1)
            def _():
                for m in span(i):
                    vpre[g, m] = decay(vdp, s, h, m) * vin[s, g, m] + vpre[g, m]

    def finish_rows(g):
        h, k = g // nk, g % nk
        first = pl.multiple_of(k * GROUP, GROUP)
        carried = [vpre[g, m] for m in range(modes)]

        def correct(t, carry):
            at = pl.ds(h * size + t * pitch + first, GROUP)
            here = lead[0, h, pl.ds(pl.multiple_of(t * modes, modes), modes), :]
            y = out[at, :] + total([here[m:m + 1, :] * carried[m] for m in range(modes)])
            act = twice_gelu(y).astype(jnp.bfloat16)
            out[at, :] = act.astype(jnp.float32)
            return carry

        lax.fori_loop(0, rows, correct, 0, unroll=32)
        p, q = spread(ptab, 1, h), spread(qtab, 1, h)

        def group(j, carry):
            c = h * nr + j
            base = h * size + j * (GROUP * pitch) + first

            def step(t, state):
                at = pl.ds(base + t, GROUP, stride=pitch)
                u = out[at, :]
                state = tuple(p[m] * state[m] + u for m in range(modes))
                out[at, :] = total([q[m] * state[m] for m in range(modes)])
                return state

            state = lax.fori_loop(0, GROUP, step, tuple(hedge[c, m] for m in range(modes)), unroll=16)
            for m in range(modes):
                hedge[c, m] = state[m]

            if pair == 2:
                @pl.when(both(k == nk - 1, jnp.logical_not(owner(c))))
                def _():
                    join_copy(c).start()

            return carry

        lax.fori_loop(0, nr, group, 0)

    def join(c):
        h = c // nr

        @pl.when(owner(c))
        def _():
            if pair == 2:
                join_copy(c).wait_recv()
            for m in range(modes):
                mine = hedge[c, m]
                if pair == 2:
                    theirs = hpart[c, m]
                    older = jnp.where(core == 0, mine, theirs)
                    newer = jnp.where(core == 0, theirs, mine)
                    mine = decay(hdt, 0, h, m) * older + newer
                hsum[c, m] = mine
            if nz > 1:
                @pl.when(z == 0)
                def _():
                    for i in range(HOPS):
                        hop_copy(c, i).start()
            if pair == 2:
                @pl.when(col == 0)
                def _():
                    forward_copy(hedge, c).start()

    def enter(c):
        h = c // nr

        @pl.when(both(owner(c), z > 0))
        def _():
            for i in range(HOPS):
                part = range(i * (modes // HOPS), (i + 1) * (modes // HOPS))
                hop_copy(c, i).wait_recv()

                @pl.when(z < nz - 1)
                def _():
                    for m in part:
                        hsum[c, m] = decay(hdt, 1, h, m) * hin[c, m] + hsum[c, m]
                    hop_copy(c, i).start()

            if pair == 2:
                @pl.when(core == 0)
                def _():
                    for m in range(modes):
                        hpart[c, m] = decay(hdt, 0, h, m) * hin[c, m] + hedge[c, m]
                    forward_copy(hpart, c).start()
                    for m in range(modes):
                        hcar[c, m] = hin[c, m]

                @pl.when(core == 1)
                def _():
                    forward_copy(hin, c).start()
                    for m in range(modes):
                        hcar[c, m] = decay(hdt, 0, h, m) * hin[c, m] + hpart[c, m]
            else:
                for m in range(modes):
                    hcar[c, m] = hin[c, m]

        if pair == 2:
            @pl.when(both(owner(c), col == 1))
            def _():
                for m in range(modes):
                    hcar[c, m] = hpart[c, m]

            @pl.when(both(jnp.logical_not(owner(c)), col > 0))
            def _():
                forward_copy(hin, c).wait_recv()
                for m in range(modes):
                    hcar[c, m] = hfwd[c, m]

    def finish_cols(c):
        h, j = c // nr, c % nr

        @pl.when(col > 0)
        def _():
            carried = [hcar[c, m] for m in range(modes)]
            base = h * size + j * (GROUP * pitch)

            def correct(t, carry):
                at = pl.ds(base + t, GROUP, stride=pitch)
                here = lead[1, h, pl.ds(pl.multiple_of(t * modes, modes), modes), :]
                out[at, :] = out[at, :] + total([here[m:m + 1, :] * carried[m] for m in range(modes)])
                return carry

            lax.fori_loop(0, cols, correct, 0, unroll=32)

    def mlp(i):
        line = jnp.concatenate(
            [
                jnp.concatenate([out[pl.ds(h * size + (i * BLOCK + r) * pitch, cols), :] for h in range(halves)], axis=1)
                for r in range(BLOCK)
            ],
            axis=0,
        )
        scale = lax.rsqrt(jnp.mean(line * line, axis=-1, keepdims=True) + 1e-06)
        normed = (line * scale).astype(jnp.bfloat16)
        pre = jnp.dot(normed, w_in[...], preferred_element_type=jnp.float32).astype(jnp.bfloat16)
        hidden = twice_gelu(pre)
        result = line + 0.5 * jnp.dot(hidden, w_out[...], preferred_element_type=jnp.float32)
        half[pl.ds(pl.multiple_of(i * (BLOCK * cols), BLOCK * cols), BLOCK * cols), :] = result.astype(half.dtype)

    hedge[...] = jnp.zeros_like(hedge)
    vpre[...] = jnp.zeros_like(vpre)

    def scan(s, carry):
        local(s)

        @pl.when(s == 0)
        def _():
            pl.semaphore_wait(barrier, sum(jnp.where(there, 1, 0) for there, _ in neighbours))

        if steps:
            @pl.when(later(0))
            def _():
                for i in range(PIECES):
                    vcopy(0, s, i).start()

            @pl.when(s >= chunks - AHEAD)
            def _():
                exchange(0, s - (chunks - AHEAD))

        return carry

    lax.fori_loop(0, chunks, scan, 0)
    fill_lead()

    def main(g, carry):
        for s in range(1, steps):
            exchange(s, g)
        finish_rows(g)
        if steps:
            @pl.when(g + AHEAD < chunks)
            def _():
                exchange(0, g + AHEAD)

        @pl.when(both(g % nk == 0, g > 0))
        def _():
            each(0, nr, lambda j: join((g // nk - 1) * nr + j))

        return carry

    def each(first, last, act):
        def go(c, carry):
            act(c)
            return carry

        lax.fori_loop(first, last, go, 0)

    lax.fori_loop(0, chunks, main, 0)

    def turn(n):
        turns = nr // pair
        return (n // nr) * nr + pair * (n % turns) + (core + (n % nr) // turns) % pair

    each(0, early, lambda n: enter(turn(n)))
    each(early, strips, lambda n: join(turn(n)))
    each(0, early, lambda n: finish_cols(turn(n)))
    for copy in fetches[4:]:
        copy.wait()

    @pl.when(z < nz - 1)
    def _():
        each(early, strips, lambda n: enter(turn(n)))

    def last(n):
        c = turn(n)

        @pl.when(z == nz - 1)
        def _():
            enter(c)

        finish_cols(c)
        per = GROUP // BLOCK
        each((c - early) * per, (c - early + 1) * per, mlp)

    each(early, strips, last)

    for s in range(steps):
        @pl.when(later(s))
        def _():
            each(0, chunks * PIECES, lambda n: vcopy(s, n // PIECES, n % PIECES).wait_send())

    def drain(c):
        if nz > 1:
            @pl.when(both(owner(c), z < nz - 1))
            def _():
                for i in range(HOPS):
                    hop_copy(c, i).wait_send()

        if pair == 2:
            @pl.when(jnp.logical_not(owner(c)))
            def _():
                join_copy(c).wait_send()

            @pl.when(both(owner(c), col != 1))
            def _():
                forward_copy(hin, c).wait_send()

    each(0, strips, drain)


def log_two(count):
    steps = count.bit_length() - 1
    assert count == 1 << steps
    return steps


def pair_of(ncol):
    return 2 if ncol % 2 == 0 else 1


def emit(src, dst, sem):
    rows = src.shape[0] // PARTS
    copies = [
        pltpu.make_async_copy(src.at[pl.ds(i * rows, rows)], dst.at[pl.ds(i * rows, rows)], sem.at[i])
        for i in range(PARTS)
    ]
    for copy in copies:
        copy.start()
    for copy in copies:
        copy.wait()


def on_device(nrow, ncol, image, vert_rate, vert_coef, horiz_rate, horiz_coef, w_in, w_out):
    rows, cols, channels = image.shape
    modes = vert_rate.shape[0]
    halves = channels // LANES
    chunks, strips = halves * (cols // GROUP), halves * (rows // GROUP)
    steps = max(log_two(nrow), 1)
    f32 = jnp.float32
    args = (image, vert_rate, vert_coef, horiz_rate, horiz_coef, w_in, w_out)
    half = pl.pallas_call(
        functools.partial(layer_kernel, nrow, ncol, rows, cols, modes, halves),
        out_shape=pltpu.VMEM((rows * cols, channels), jnp.bfloat16),
        in_specs=[pl.BlockSpec(memory_space=pltpu.MemorySpace.HBM)] * len(args),
        out_specs=pl.BlockSpec(memory_space=pltpu.MemorySpace.VMEM),
        scratch_shapes=[pltpu.VMEM(a.shape, a.dtype) for a in args] + [
            pltpu.VMEM((halves * rows * (cols + 1), LANES), f32),
            pltpu.VMEM((2, halves, modes, LANES), f32),
            pltpu.VMEM((2, halves, modes, LANES), f32),
            pltpu.VMEM((steps, halves, modes, LANES), f32),
            pltpu.VMEM((steps, halves, modes, LANES), f32),
            pltpu.VMEM((2, halves, modes, LANES), f32),
            pltpu.VMEM((2, halves, max(rows, cols) * modes, LANES), f32),
            pltpu.VMEM((steps, chunks, modes, GROUP, LANES), f32),
            pltpu.VMEM((steps, chunks, modes, GROUP, LANES), f32),
            pltpu.VMEM((chunks, modes, GROUP, LANES), f32),
        ] + [pltpu.VMEM((strips, modes, GROUP, LANES), f32)] * 6 + [
            pltpu.SemaphoreType.DMA((steps, chunks * PIECES)),
            pltpu.SemaphoreType.DMA((steps, chunks * PIECES)),
            pltpu.SemaphoreType.DMA((strips,)),
            pltpu.SemaphoreType.DMA((strips,)),
            pltpu.SemaphoreType.DMA((strips * HOPS,)),
            pltpu.SemaphoreType.DMA((strips * HOPS,)),
            pltpu.SemaphoreType.DMA((strips,)),
            pltpu.SemaphoreType.DMA((strips,)),
            pltpu.SemaphoreType.DMA((chunks,)),
            pltpu.SemaphoreType.DMA((6,)),
        ],
        compiler_params=pltpu.CompilerParams(collective_id=0, has_side_effects=True, vmem_limit_bytes=67043328 - rows * cols * channels * 2 - 4096),
    )(*args)
    full = pl.pallas_call(
        emit, out_shape=jax.ShapeDtypeStruct((rows * cols, channels), jnp.bfloat16),
        in_specs=[pl.BlockSpec(memory_space=pltpu.MemorySpace.VMEM)],
        out_specs=pl.BlockSpec(memory_space=pltpu.MemorySpace.HBM),
        scratch_shapes=[pltpu.SemaphoreType.DMA((PARTS,))],
        compiler_params=pltpu.CompilerParams(vmem_limit_bytes=1000000),
    )(half)
    return full.reshape(rows, cols, channels)


def solution(mesh):
    placed = (P("row", "col", None), P(), P(), P(), P(), P(), P())
    return jax.shard_map(
        functools.partial(on_device, mesh.shape["row"], mesh.shape["col"]),
        mesh=mesh, in_specs=placed, out_specs=P("row", "col", None), check_vma=False,
    )
```
